32 devices in a mesh: row: 8 (over y, x, core), col: 4 (over z).
Axes of the slice: x: 2, y: 2, z: 4, core: 2. Of those that a mesh axis runs over, the one named last changes fastest.
Arguments:
- features: bfloat16 [512, 128, 128], P('row', 'col'), may hold values from -6 to 6
- cotangent: bfloat16 [512, 128, 128], P('row', 'col'), may hold values from -6 to 6
- kernels: bfloat16 [2, 9, 128, 128], replicated, may hold values from -0.1875 to 0.1875
- momentum: float32 [2, 147456], replicated, may hold values from -6 to 6
- mlp_in_weight: float32 [32, 3], replicated, may hold values from -3.5 to 3.5
- mlp_in_bias: float32 [32], replicated, may hold values from -3 to 3
- mlp_out_weight: float32 [2, 32], replicated, may hold values from -1 to 1
- mlp_out_bias: float32 [2], replicated, may hold values from -3 to 3
Outputs:
- update: float32 [2, 147456], replicated
- momentum_out: float32 [2, 147456], replicated
The draws below stay inside these ranges and needn't reach their ends.
All inputs are finite; a program needn't handle non-finite values.
Results may differ from the reference program's by a relative error of at most 0.0014.
Values may be sent and summed in bfloat16 or wider, within the bound.
A program may use at most 64 MiB of HBM per device.

```python
import math
import jax
import jax.numpy as jnp
from jax import lax

C = 128
MLP_HID = 32
H = 512
W = 128
KP = 147456


def block_levels(stream_key, shape, pieces, low, high):
    level = 1.0
    for axis_at, shards_of in pieces:
        heights = jax.random.uniform(jax.random.fold_in(jax.random.fold_in(stream_key, 6), axis_at), (shards_of,), jnp.float32, low / len(pieces), high / len(pieces))
        level = level * jnp.repeat(jnp.exp(heights), shape[axis_at] // shards_of).reshape((-1,) + (1,) * (len(shape) - 1 - axis_at))
    return level


def scatter_about(stream_key, shape, width, limit, shards=(), kind=jnp.bfloat16):
    entries = jax.random.normal(stream_key, shape, jnp.float32) * width
    if len(shards) > 0:
        entries = block_levels(stream_key, shape, shards, -0.22, 0.18) * entries
    return jnp.clip(entries, min=-limit, max=limit).astype(kind)


def setup_inputs(seed: int = 0) -> dict:
    key_of = jax.random.split(jax.random.key(seed), 9)
    features = scatter_about(key_of[0], (H, W, C), 1.0, 6.0, ((0, 8), (1, 4)))
    cotangent = scatter_about(key_of[1], (H, W, C), 1.0, 6.0, ((0, 8), (1, 4)))
    kernels = scatter_about(key_of[2], (2, 9, C, C), (9 * C) ** -0.5, 0.1875)
    momentum = scatter_about(key_of[3], (2, KP), 1.0, 6.0, (), jnp.float32)
    mlp_in_weight = scatter_about(key_of[4], (MLP_HID, 3), 3 ** -0.5, 3.5, (), jnp.float32)
    mlp_in_bias = scatter_about(key_of[5], (MLP_HID,), 0.5, 3.0, (), jnp.float32)
    mlp_out_weight = scatter_about(key_of[6], (2, MLP_HID), MLP_HID ** -0.5, 1.0, (), jnp.float32)
    mlp_out_bias = scatter_about(key_of[7], (2,), 0.5, 3.0, (), jnp.float32)
    return dict(features=features, cotangent=cotangent, kernels=kernels, momentum=momentum, mlp_in_weight=mlp_in_weight, mlp_in_bias=mlp_in_bias, mlp_out_weight=mlp_out_weight, mlp_out_bias=mlp_out_bias)


def convolve(image, kernel):
    summed = jnp.zeros((H * W, C), jnp.float32)
    for tap_row in range(3):
        for tap_col in range(3):
            moved = jnp.roll(image, (1 - tap_row, 1 - tap_col), axis=(0, 1)).reshape(H * W, C)
            summed = summed + jnp.dot(moved, kernel[3 * tap_row + tap_col], preferred_element_type=jnp.float32)
    return summed.reshape(H, W, C)

def kernel_grad(image, cotangent):
    flat_cot = cotangent.reshape(H * W, C)
    taps = []
    for tap_row in range(3):
        for tap_col in range(3):
            moved = jnp.roll(image, (1 - tap_row, 1 - tap_col), axis=(0, 1)).reshape(H * W, C)
            taps.append(lax.dot_general(moved, flat_cot, (((0,), (0,)), ((), ())), preferred_element_type=jnp.float32))
    return jnp.stack(taps)

def transpose_conv(cotangent, kernel):
    summed = jnp.zeros((H * W, C), jnp.float32)
    for tap_row in range(3):
        for tap_col in range(3):
            moved = jnp.roll(cotangent, (tap_row - 1, tap_col - 1), axis=(0, 1)).reshape(H * W, C)
            summed = summed + lax.dot_general(moved, kernel[3 * tap_row + tap_col], (((1,), (1,)), ((), ())), preferred_element_type=jnp.float32)
    return summed.reshape(H, W, C)

def learned_step(grads, squares, momentum, weights, w_in, b_in, w_out, b_out, gain, count):
    norm_scale = 1.0 / jnp.sqrt(squares / count + 1e-06)
    g_hat = grads * norm_scale[:, None]
    momentum_new = 0.9 * momentum + 0.1 * g_hat
    scaled = weights.astype(jnp.float32) * gain
    pre_units = w_in[:, 0][:, None, None] * g_hat[None] + w_in[:, 1][:, None, None] * momentum_new[None]
    pre_units = pre_units + w_in[:, 2][:, None, None] * scaled[None] + b_in[:, None, None]
    units = jax.nn.silu(pre_units)
    mlp_result = jnp.einsum('kh,hlp->klp', w_out, units, precision=lax.Precision.HIGHEST) + b_out[:, None, None]
    update = mlp_result[0] * jnp.exp(jnp.tanh(mlp_result[1]))
    return (update, momentum_new)

def reference(features, cotangent, kernels, momentum, mlp_in_weight, mlp_in_bias, mlp_out_weight, mlp_out_bias):
    pre_act = convolve(features, kernels[0])
    hidden = jax.nn.silu(pre_act).astype(jnp.bfloat16)
    grad_two = kernel_grad(hidden, cotangent)
    back_grad = transpose_conv(cotangent, kernels[1])
    sigma_val = jax.nn.sigmoid(pre_act)
    pre_grad = (back_grad * sigma_val * (1.0 + pre_act * (1.0 - sigma_val))).astype(jnp.bfloat16)
    grad_one = kernel_grad(features, pre_grad)
    grads = jnp.stack([grad_one.reshape(-1), grad_two.reshape(-1)])
    squares = lax.optimization_barrier(jnp.sum(grads * grads, axis=1))
    weights = kernels.reshape(2, KP)
    update, momentum_new = learned_step(grads, squares, momentum, weights, mlp_in_weight, mlp_in_bias, mlp_out_weight, mlp_out_bias, math.sqrt(9.0 * C), float(KP))
    return (update, momentum_new)
```

```python
import functools
import math

import jax
import jax.numpy as jnp
from jax import lax
from jax.experimental import pallas as pl
from jax.experimental.pallas import tpu as pltpu
from jax.sharding import PartitionSpec as P

MESH = pl.DeviceIdType.MESH
TILE = 8
F32 = jnp.float32
BF16 = jnp.bfloat16


def plan(rows_axis, cols_axis, channels):
    bits = rows_axis.bit_length() - 1
    owners = (rows_axis // 2) * cols_axis
    true = (5 * channels, 4 * channels)
    padded = tuple(-(-t // (owners * TILE)) * owners * TILE for t in true)
    orders = (tuple(range(1, bits)), tuple(reversed(range(1, bits))))
    chunks = tuple(p // owners for p in padded)
    return true, padded, orders, chunks


def place(row, order, total):
    off = 0
    for bit in order:
        total //= 2
        off = off + ((row // 2**bit) % 2) * total
    return off


def step_kernel(
    cfg,
    feat, cot, ker, mw, w_in, b_in, w_out, b_out,
    grads_out, upd_out, sq_out,
    edge, ns, we, cr, x3, y3, hid, pg, g, rc, s, rb, zb, sq,
    halo_send, halo_recv, rs_send, rs_recv, z_send, z_recv, sq_send, sq_recv,
    ag_send, ag_recv, agz_send, agz_recv,
):
    rows_axis, cols_axis, param_count, true, padded, orders, chunks = cfg
    tile_rows, tile_cols, ch = feat.shape
    cells = tile_rows * tile_cols
    row, col = lax.axis_index("row"), lax.axis_index("col")
    core = row % 2
    other = row + 1 - 2 * core
    devices = rows_axis * cols_axis
    base = (0, padded[0])

    def remote(src, dst, send, recv, to):
        return pltpu.make_async_remote_copy(
            src_ref=src, dst_ref=dst, send_sem=send, recv_sem=recv,
            device_id=to, device_id_type=MESH,
        )

    for i, ref in enumerate((feat, cot)):
        edge[i, 0] = ref[:, 0:16, :].astype(F32)[:, 0, :].astype(BF16)
        edge[i, 1] = ref[:, tile_cols - 16 :, :].astype(F32)[:, 15, :].astype(BF16)

    barrier = pltpu.get_barrier_semaphore()
    here = row * cols_axis + col

    def greet(d, carry):
        t = (here + d) % devices
        pl.semaphore_signal(
            barrier, inc=1, device_id=(t // cols_axis, t % cols_axis), device_id_type=MESH
        )
        return carry

    lax.fori_loop(1, devices, greet, 0)
    pl.semaphore_wait(barrier, devices - 1)

    up, down = (row + rows_axis - 1) % rows_axis, (row + 1) % rows_axis
    west, east = (col + cols_axis - 1) % cols_axis, (col + 1) % cols_axis
    last = tile_rows - 1
    halos = []
    for i, ref in enumerate((feat, cot)):
        lo, hi = pl.ds(0, 16), pl.ds(tile_cols - 16, 16)
        moves = (
            (ref.at[last], ns.at[i, 0], (down, col)),
            (ref.at[0], ns.at[i, 1], (up, col)),
            (edge.at[i, 1], we.at[i, 0], (row, east)),
            (edge.at[i, 0], we.at[i, 1], (row, west)),
            (ref.at[last, hi], cr.at[i, 0], (down, east)),
            (ref.at[last, lo], cr.at[i, 1], (down, west)),
            (ref.at[0, hi], cr.at[i, 2], (up, east)),
            (ref.at[0, lo], cr.at[i, 3], (up, west)),
        )
        mine = [
            remote(src, dst, halo_send.at[i, k], halo_recv.at[i, k], to)
            for k, (src, dst, to) in enumerate(moves)
        ]
        for copy in mine:
            copy.start()
        halos.append(mine)

    def put(dst, first, v, w, e):
        n = v.shape[0]
        at = lax.broadcasted_iota(jnp.int32, v.shape, 1)
        left = jnp.where(at == 0, w[:, None, :], pltpu.roll(v, 1, 1))
        right = jnp.where(at == tile_cols - 1, e[:, None, :], pltpu.roll(v, tile_cols - 1, 1))
        span = pl.ds(first * tile_cols, n * tile_cols)
        for b, part in enumerate((left, v, right)):
            dst[span, b * ch : (b + 1) * ch] = part.reshape(n * tile_cols, ch).astype(BF16)

    def build(i, ref, dst):
        for copy in halos[i]:
            copy.wait_recv()
        put(dst, 0, ns[i, 0].astype(F32)[None], cr[i, 0].astype(F32)[15:16], cr[i, 1].astype(F32)[0:1])
        for r in range(0, tile_rows, 16):
            span = pl.ds(r, 16)
            put(dst, r + 1, ref[span].astype(F32), we[i, 0, span].astype(F32), we[i, 1, span].astype(F32))
        put(
            dst, tile_rows + 1,
            ns[i, 1].astype(F32)[None], cr[i, 2].astype(F32)[15:16], cr[i, 3].astype(F32)[0:1],
        )

    build(0, feat, x3)
    build(1, cot, y3)

    flip = [
        jnp.concatenate([ker[1, (3 * a + b) * ch : (3 * a + b + 1) * ch] for b in (2, 1, 0)], axis=1)
        for a in range(3)
    ]
    block = min(cells, 512)
    for m in range(0, cells, block):
        pre = jnp.zeros((block, ch), F32)
        back = jnp.zeros((block, ch), F32)
        for a in range(3):
            pre += jnp.dot(
                x3[pl.ds(m + a * tile_cols, block)],
                ker[0, 3 * a * ch : 3 * (a + 1) * ch],
                preferred_element_type=F32,
            )
            back += lax.dot_general(
                y3[pl.ds(m + (2 - a) * tile_cols, block)], flip[a],
                (((1,), (1,)), ((), ())), preferred_element_type=F32,
            )
        sig = 1.0 / (1.0 + jnp.exp(-pre))
        hid[pl.ds(m, block)] = (pre * sig).astype(BF16)
        pg[pl.ds(m, block)] = (back * sig * (1.0 + pre * (1.0 - sig))).astype(BF16)

    def tap_rows(t):
        return pl.ds(t * ch if t < 5 else padded[0] + (t - 5) * ch, ch)

    for part in range(2):
        gap = padded[part] - true[part]
        if gap:
            for layer in range(2):
                g[layer, pl.ds(base[part] + true[part], gap)] = jnp.zeros((gap, ch), F32)

    hid_t, pg_t = hid[...].T, pg[...].T
    for a in range(3):
        two = jnp.dot(hid_t, y3[pl.ds((2 - a) * tile_cols, cells)], preferred_element_type=F32)
        one = jnp.dot(pg_t, x3[pl.ds(a * tile_cols, cells)], preferred_element_type=F32)
        for b in range(3):
            g[1, tap_rows(3 * a + 2 - b)] = two[:, b * ch : (b + 1) * ch]
            g[0, tap_rows(3 * a + b)] = one[:, b * ch : (b + 1) * ch].T

    sent = [copy for mine in halos for copy in mine]
    waits = []
    for part in range(2):
        span = pl.ds(base[part], padded[part])
        copy = remote(
            g.at[1 - core, span], rc.at[span],
            rs_send.at[part, 0], rs_recv.at[part, 0], (other, col),
        )
        copy.start()
        waits.append(copy)
    sent += waits
    off, size, slot = list(base), list(padded), list(base)
    steps = len(orders[0])
    pending = [None, None]

    def begin(part, step):
        bit = orders[part][step]
        side = (row // 2**bit) % 2
        size[part] //= 2
        n = size[part]
        away = pl.multiple_of(off[part] + (1 - side) * n, TILE)
        off[part] = off[part] + side * n
        into = pl.ds(slot[part], n)
        slot[part] += n
        copy = remote(
            s.at[pl.ds(away, n)], rb.at[into],
            rs_send.at[part, step + 1], rs_recv.at[part, step + 1],
            (row + (1 - 2 * side) * 2**bit, col),
        )
        copy.start()
        sent.append(copy)
        pending[part] = (copy, into, n)

    for part in range(2):
        waits[part].wait_recv()
        span = pl.ds(base[part], padded[part])
        s[span] = g[core, span] + rc[span]
        begin(part, 0)
    for step in range(steps):
        for part in range(2):
            copy, into, n = pending[part]
            copy.wait_recv()
            span = pl.ds(pl.multiple_of(off[part], TILE), n)
            s[span] += rb[into]
            if step + 1 < steps:
                begin(part, step + 1)
            else:
                for d in range(1, cols_axis):
                    to = (col + d) % cols_axis
                    n = chunks[part]
                    c = remote(
                        s.at[pl.ds(pl.multiple_of(off[part] + to * n, TILE), n)],
                        zb.at[d, pl.ds(0 if part == 0 else chunks[0], n)],
                        z_send.at[part, d], z_recv.at[part, d], (row, to),
                    )
                    c.start()
                    sent.append(c)
                    pending[part] = (pending[part] if d > 1 else ()) + (c,)

    own = []
    mine = []
    for part in range(2):
        n = chunks[part]
        at = pl.ds(pl.multiple_of(off[part] + col * n, TILE), n)
        total = s[at]
        for d in range(1, cols_axis):
            pending[part][d - 1].wait_recv()
            total += zb[d, pl.ds(0 if part == 0 else chunks[0], n)]
        grads_out[core, at] = total
        own.append(at)
        mine.append(total)

    both = jnp.concatenate(mine, axis=0)
    count = chunks[0] + chunks[1]
    sq[0] = jnp.sum((both * both).reshape(count // TILE, TILE, ch), axis=0)
    owners = (rows_axis // 2) * cols_axis
    me = (row // 2) * cols_axis + col

    def sq_copy(d):
        t = (me + d) % owners
        return remote(
            sq.at[0], sq.at[d], sq_send.at[d], sq_recv.at[d],
            (2 * (t // cols_axis) + core, t % cols_axis),
        )

    def sq_start(d, carry):
        sq_copy(d).start()
        return carry

    lax.fori_loop(1, owners, sq_start, 0)

    def spread_col(k, out):
        copies = []
        for part in range(2):
            for d in range(1, cols_axis):
                c = remote(
                    out.at[core, own[part]], out.at[core, own[part]],
                    agz_send.at[k, part, d], agz_recv.at[k, part, d],
                    (row, (col + d) % cols_axis),
                )
                c.start()
                sent.append(c)
                copies.append((part, c))
        return copies

    outs = (grads_out, upd_out)
    flight = [spread_col(0, grads_out), None]

    def sq_wait(d, tot):
        sq_copy(d).wait_recv()
        return tot + sq[d]

    total = lax.fori_loop(1, owners, sq_wait, sq[0])
    total = jnp.broadcast_to(jnp.sum(total, axis=(0, 1), keepdims=True), (TILE, ch))
    sq_out[core] = total

    norm = 1.0 / jnp.sqrt(total[0:1] / param_count + 1e-06)
    g_hat = both * norm
    mom = 0.9 * mw[0] + 0.1 * g_hat
    scaled = mw[1]

    def unit(h, carry):
        r0, r1 = carry
        v = w_in[h, 0] * g_hat + w_in[h, 1] * mom
        v = v + w_in[h, 2] * scaled + b_in[h]
        u = v * (1.0 / (1.0 + jnp.exp(-v)))
        return r0 + w_out[0, h] * u, r1 + w_out[1, h] * u

    zero = jnp.zeros((count, ch), F32)
    r0, r1 = lax.fori_loop(0, b_in.shape[0], unit, (zero, zero), unroll=4)
    update = (r0 + b_out[0]) * jnp.exp(jnp.tanh(r1 + b_out[1]))
    upd_out[core, own[0]] = update[: chunks[0]]
    upd_out[core, own[1]] = update[chunks[0] :]
    flight[1] = spread_col(1, upd_out)

    sq_final = remote(
        sq_out.at[core], sq_out.at[core], sq_send.at[0], sq_recv.at[0], (other, col)
    )
    sq_final.start()
    sent.append(sq_final)

    offs = [list(off), list(off)]
    sizes = [list(size), list(size)]
    for step in range(steps + 1):
        for k, out in enumerate(outs):
            copies = []
            for part in range(2):
                for p, c in flight[k]:
                    if p == part:
                        c.wait_recv()
                n = sizes[k][part]
                if step < steps:
                    bit = orders[part][steps - 1 - step]
                    side = (row // 2**bit) % 2
                    to = (row + (1 - 2 * side) * 2**bit, col)
                    at = pl.ds(pl.multiple_of(offs[k][part], TILE), n)
                    offs[k][part] = offs[k][part] - side * n
                    sizes[k][part] = 2 * n
                else:
                    to = (other, col)
                    at = pl.ds(base[part], n)
                c = remote(
                    out.at[core, at], out.at[core, at],
                    ag_send.at[k, part, step], ag_recv.at[k, part, step], to,
                )
                c.start()
                sent.append(c)
                copies.append((part, c))
            flight[k] = copies
    for k in range(2):
        for _, c in flight[k]:
            c.wait_recv()
    sq_final.wait_recv()
    for c in sent:
        c.wait_send()

    def sq_done(d, carry):
        sq_copy(d).wait_send()
        return carry

    lax.fori_loop(1, owners, sq_done, 0)


def on_device(
    rows_axis, cols_axis,
    features, cotangent, kernels, momentum, mlp_in_weight, mlp_in_bias, mlp_out_weight, mlp_out_bias,
):
    tile_rows, tile_cols, ch = features.shape
    param_count = 9 * ch * ch
    gain = math.sqrt(9.0 * ch)
    true, padded, orders, chunks = plan(rows_axis, cols_axis, ch)
    row, col = lax.axis_index("row"), lax.axis_index("col")
    steps = len(orders[0])
    owners = (rows_axis // 2) * cols_axis
    length = sum(padded)

    def shard(values):
        pieces, first = [], 0
        for part in range(2):
            size = true[part] * ch
            cut = values[:, first : first + size]
            cut = jnp.pad(cut, ((0, 0), (0, padded[part] * ch - size)))
            at = (place(row, orders[part], padded[part]) + col * chunks[part]) * ch
            piece = lax.dynamic_slice(cut, (row % 2, at), (1, chunks[part] * ch))
            pieces.append(piece.reshape(chunks[part], ch))
            first += size
        return jnp.concatenate(pieces, axis=0).astype(F32)

    mw = jnp.stack([shard(momentum), shard(kernels.reshape(2, param_count)) * gain])
    cfg = (rows_axis, cols_axis, float(param_count), true, padded, orders, chunks)
    vmem = pl.BlockSpec(memory_space=pltpu.VMEM)
    smem = pl.BlockSpec(memory_space=pltpu.SMEM)
    dma = pltpu.SemaphoreType.DMA
    full = (length, ch)
    grads, update, squares = pl.pallas_call(
        functools.partial(step_kernel, cfg),
        out_shape=(
            jax.ShapeDtypeStruct((2,) + full, F32),
            jax.ShapeDtypeStruct((2,) + full, F32),
            jax.ShapeDtypeStruct((2, TILE, ch), F32),
        ),
        in_specs=[vmem] * 4 + [smem] * 4,
        out_specs=(vmem,) * 3,
        scratch_shapes=[
            pltpu.VMEM((2, 2, tile_rows, ch), BF16),
            pltpu.VMEM((2, 2, tile_cols, ch), BF16),
            pltpu.VMEM((2, 2, tile_rows, ch), BF16),
            pltpu.VMEM((2, 4, 16, ch), BF16),
            pltpu.VMEM(((tile_rows + 2) * tile_cols, 3 * ch), BF16),
            pltpu.VMEM(((tile_rows + 2) * tile_cols, 3 * ch), BF16),
            pltpu.VMEM((tile_rows * tile_cols, ch), BF16),
            pltpu.VMEM((tile_rows * tile_cols, ch), BF16),
            pltpu.VMEM((2,) + full, F32),
            pltpu.VMEM(full, F32),
            pltpu.VMEM(full, F32),
            pltpu.VMEM(full, F32),
            pltpu.VMEM((cols_axis, sum(chunks), ch), F32),
            pltpu.VMEM((owners, TILE, ch), F32),
            dma((2, 8)), dma((2, 8)),
            dma((2, steps + 1)), dma((2, steps + 1)),
            dma((2, cols_axis)), dma((2, cols_axis)),
            dma((owners,)), dma((owners,)),
            dma((2, 2, steps + 1)), dma((2, 2, steps + 1)),
            dma((2, 2, cols_axis)), dma((2, 2, cols_axis)),
        ],
        compiler_params=pltpu.CompilerParams(
            collective_id=0, has_side_effects=True, vmem_limit_bytes=48 * 2**20
        ),
    )(
        features, cotangent, kernels.reshape(2, 9 * ch, ch), mw,
        mlp_in_weight, mlp_in_bias, mlp_out_weight, mlp_out_bias,
    )

    def flat(values):
        if padded != true:
            values = jnp.concatenate(
                [values[:, : true[0]], values[:, padded[0] : padded[0] + true[1]]], axis=1
            )
        return values.reshape(2, param_count)

    norm = 1.0 / jnp.sqrt(squares[:, 0, :1] / float(param_count) + 1e-06)
    momentum_out = 0.9 * momentum + 0.1 * (flat(grads) * norm)
    return flat(update), momentum_out


def solution(mesh):
    placed = (P("row", "col", None), P("row", "col", None), P(), P(), P(), P(), P(), P())
    return jax.shard_map(
        functools.partial(on_device, mesh.shape["row"], mesh.shape["col"]),
        mesh=mesh, in_specs=placed, out_specs=(P(), P()), check_vma=False,
    )
```

```python
import functools
import math

import jax
import jax.numpy as jnp
from jax import lax
from jax.experimental import pallas as pl
from jax.experimental.pallas import tpu as pltpu
from jax.sharding import PartitionSpec as P

MESH = pl.DeviceIdType.MESH
TILE = 8
F32 = jnp.float32
BF16 = jnp.bfloat16


def plan(rows_axis, cols_axis, channels):
    bits = rows_axis.bit_length() - 1
    owners = (rows_axis // 2) * cols_axis
    true = 3 * channels
    padded = -(-true // (owners * TILE)) * owners * TILE
    stages = list(range(1, bits)) + [None]
    orders = tuple(tuple(stages[p:] + stages[:p]) for p in (0, 1, len(stages) - 1))
    return true, padded, orders, padded // owners


def place(row, col, cols_axis, order, total):
    off = 0
    for bit in order:
        if bit is None:
            total //= cols_axis
            off = off + col * total
        else:
            total //= 2
            off = off + ((row // 2**bit) % 2) * total
    return off


def step_kernel(
    cfg,
    feat, cot, ker, mw, w_in, b_in, w_out, b_out,
    grads_flat, upd_flat, sq_out,
    edge, ns, we, cr, x3, y3, hid, pg, g, rc, s, rb, sq, grads_out, upd_out,
    halo_send, halo_recv, core_send, core_recv, rs_send, rs_recv, sq_send, sq_recv,
    ag_send, ag_recv, fw_send, fw_recv,
):
    rows_axis, cols_axis, param_count, true, padded, orders, chunk = cfg
    tile_rows, tile_cols, ch = feat.shape
    cells = tile_rows * tile_cols
    row, col = lax.axis_index("row"), lax.axis_index("col")
    core = row % 2
    other = row + 1 - 2 * core
    devices = rows_axis * cols_axis
    base = (0, padded, 2 * padded)
    parts = range(3)

    def remote(src, dst, send, recv, to):
        return pltpu.make_async_remote_copy(
            src_ref=src, dst_ref=dst, send_sem=send, recv_sem=recv,
            device_id=to, device_id_type=MESH,
        )

    for i, ref in enumerate((feat, cot)):
        edge[i, 0] = ref[:, 0:16, :].astype(F32)[:, 0, :].astype(BF16)
        edge[i, 1] = ref[:, tile_cols - 16 :, :].astype(F32)[:, 15, :].astype(BF16)

    barrier = pltpu.get_barrier_semaphore()
    here = row * cols_axis + col

    def greet(d, carry):
        t = (here + d) % devices
        pl.semaphore_signal(
            barrier, inc=1, device_id=(t // cols_axis, t % cols_axis), device_id_type=MESH
        )
        return carry

    lax.fori_loop(1, devices, greet, 0)
    pl.semaphore_wait(barrier, devices - 1)

    up, down = (row + rows_axis - 1) % rows_axis, (row + 1) % rows_axis
    west, east = (col + cols_axis - 1) % cols_axis, (col + 1) % cols_axis
    last = tile_rows - 1
    halos = []
    for i, ref in enumerate((feat, cot)):
        lo, hi = pl.ds(0, 16), pl.ds(tile_cols - 16, 16)
        moves = (
            (ref.at[last], ns.at[i, 0], (down, col)),
            (ref.at[0], ns.at[i, 1], (up, col)),
            (edge.at[i, 1], we.at[i, 0], (row, east)),
            (edge.at[i, 0], we.at[i, 1], (row, west)),
            (ref.at[last, hi], cr.at[i, 0], (down, east)),
            (ref.at[last, lo], cr.at[i, 1], (down, west)),
            (ref.at[0, hi], cr.at[i, 2], (up, east)),
            (ref.at[0, lo], cr.at[i, 3], (up, west)),
        )
        mine = [
            remote(src, dst, halo_send.at[i, k], halo_recv.at[i, k], to)
            for k, (src, dst, to) in enumerate(moves)
        ]
        for copy in mine:
            copy.start()
        halos.append(mine)

    def put(dst, first, v, w, e):
        n = v.shape[0]
        at = lax.broadcasted_iota(jnp.int32, v.shape, 1)
        left = jnp.where(at == 0, w[:, None, :], pltpu.roll(v, 1, 1))
        right = jnp.where(at == tile_cols - 1, e[:, None, :], pltpu.roll(v, tile_cols - 1, 1))
        span = pl.ds(first * tile_cols, n * tile_cols)
        for b, part in enumerate((left, v, right)):
            dst[span, b * ch : (b + 1) * ch] = part.reshape(n * tile_cols, ch).astype(BF16)

    def build(i, ref, dst):
        for copy in halos[i]:
            copy.wait_recv()
        put(dst, 0, ns[i, 0].astype(F32)[None], cr[i, 0].astype(F32)[15:16], cr[i, 1].astype(F32)[0:1])
        for r in range(0, tile_rows, 16):
            span = pl.ds(r, 16)
            put(dst, r + 1, ref[span].astype(F32), we[i, 0, span].astype(F32), we[i, 1, span].astype(F32))
        put(
            dst, tile_rows + 1,
            ns[i, 1].astype(F32)[None], cr[i, 2].astype(F32)[15:16], cr[i, 3].astype(F32)[0:1],
        )

    build(0, feat, x3)
    build(1, cot, y3)

    flip = [
        jnp.concatenate([ker[1, (3 * a + b) * ch : (3 * a + b + 1) * ch] for b in (2, 1, 0)], axis=1)
        for a in range(3)
    ]
    block = min(cells, 512)
    for m in range(0, cells, block):
        pre = jnp.zeros((block, ch), F32)
        back = jnp.zeros((block, ch), F32)
        for a in range(3):
            pre += jnp.dot(
                x3[pl.ds(m + a * tile_cols, block)],
                ker[0, 3 * a * ch : 3 * (a + 1) * ch],
                preferred_element_type=F32,
            )
            back += lax.dot_general(
                y3[pl.ds(m + (2 - a) * tile_cols, block)], flip[a],
                (((1,), (1,)), ((), ())), preferred_element_type=F32,
            )
        sig = 1.0 / (1.0 + jnp.exp(-pre))
        hid[pl.ds(m, block)] = (pre * sig).astype(BF16)
        pg[pl.ds(m, block)] = (back * sig * (1.0 + pre * (1.0 - sig))).astype(BF16)

    def tap_rows(t):
        return pl.ds(base[t // 3] + (t % 3) * ch, ch)

    if padded > true:
        for part in parts:
            for layer in range(2):
                g[layer, pl.ds(base[part] + true, padded - true)] = jnp.zeros((padded - true, ch), F32)

    sent = [copy for mine in halos for copy in mine]
    swaps = []
    hid_t, pg_t = hid[...].T, pg[...].T
    for a in parts:
        two = jnp.dot(hid_t, y3[pl.ds((2 - a) * tile_cols, cells)], preferred_element_type=F32)
        one = jnp.dot(pg_t, x3[pl.ds(a * tile_cols, cells)], preferred_element_type=F32)
        for b in range(3):
            g[1, tap_rows(3 * a + 2 - b)] = two[:, b * ch : (b + 1) * ch]
            g[0, tap_rows(3 * a + b)] = one[:, b * ch : (b + 1) * ch].T
        span = pl.ds(base[a], padded)
        copy = remote(
            g.at[1 - core, span], rc.at[span], core_send.at[a], core_recv.at[a], (other, col)
        )
        copy.start()
        swaps.append(copy)
    sent += swaps

    off, size, slot = list(base), [padded] * 3, list(base)
    steps = len(orders[0])
    pending = [None] * 3

    def rows_at(start, n):
        return pl.ds(pl.multiple_of(start, TILE), n)

    def begin(part, step):
        bit = orders[part][step]
        if bit is None:
            n = size[part] // cols_axis
            peers = [
                (d, off[part] + ((col + d) % cols_axis) * n, (row, (col + d) % cols_axis))
                for d in range(1, cols_axis)
            ]
            off[part] = off[part] + col * n
        else:
            n = size[part] // 2
            side = (row // 2**bit) % 2
            peers = [(0, off[part] + (1 - side) * n, (row + (1 - 2 * side) * 2**bit, col))]
            off[part] = off[part] + side * n
        size[part] = n
        pending[part] = []
        for d, start, to in peers:
            into = pl.ds(slot[part], n)
            slot[part] += n
            copy = remote(
                s.at[rows_at(start, n)], rb.at[into],
                rs_send.at[part, step, d], rs_recv.at[part, step, d], to,
            )
            copy.start()
            sent.append(copy)
            pending[part].append((copy, into))

    for part in parts:
        swaps[part].wait_recv()
        span = pl.ds(base[part], padded)
        s[span] = g[core, span] + rc[span]
        begin(part, 0)
    own, mine = [], []
    for step in range(steps):
        for part in parts:
            at = rows_at(off[part], size[part])
            total = s[at]
            for copy, into in pending[part]:
                copy.wait_recv()
                total += rb[into]
            if step + 1 < steps:
                s[at] = total
                begin(part, step + 1)
            else:
                grads_out[core, at] = total
                own.append(at)
                mine.append(total)

    outs = (grads_out, upd_out)
    offs, sizes = [list(off), list(off)], [list(size), list(size)]
    flight = [[None] * 3, [None] * 3]
    landing = [[], []]

    def forward(k, part, step, d, at):
        c = remote(
            outs[k].at[core, at], outs[k].at[core, at],
            fw_send.at[k, part, step, d], fw_recv.at[k, part, step, d], (other, col),
        )
        c.start()
        sent.append(c)
        landing[k].append(c)

    def spread(k, part, step):
        bit = orders[part][step]
        n, first = sizes[k][part], offs[k][part]
        here_at = rows_at(first, n)
        if bit is None:
            whole = first - col * n
            peers = [
                (d, (row, (col + d) % cols_axis), whole + ((col + cols_axis - d) % cols_axis) * n)
                for d in range(1, cols_axis)
            ]
            offs[k][part], sizes[k][part] = whole, n * cols_axis
        else:
            side = (row // 2**bit) % 2
            whole = first - side * n
            peers = [(0, (row + (1 - 2 * side) * 2**bit, col), whole + (1 - side) * n)]
            offs[k][part], sizes[k][part] = whole, 2 * n
        flight[k][part] = []
        for d, to, arrives in peers:
            c = remote(
                outs[k].at[core, here_at], outs[k].at[core, here_at],
                ag_send.at[k, part, step, d], ag_recv.at[k, part, step, d], to,
            )
            c.start()
            sent.append(c)
            flight[k][part].append((c, step, d, rows_at(arrives, n)))

    def collect(k, part):
        for c, step, d, at in flight[k][part]:
            c.wait_recv()
            forward(k, part, step, d, at)

    def launch(k):
        for part in parts:
            spread(k, part, steps - 1)
        for part in parts:
            forward(k, part, steps, 0, own[part])

    both = jnp.concatenate(mine, axis=0)
    count = 3 * chunk
    sq[0] = jnp.sum((both * both).reshape(count // TILE, TILE, ch), axis=0)
    owners = (rows_axis // 2) * cols_axis
    me = (row // 2) * cols_axis + col

    def sq_copy(d):
        t = (me + d) % owners
        return remote(
            sq.at[0], sq.at[d], sq_send.at[d], sq_recv.at[d],
            (2 * (t // cols_axis) + core, t % cols_axis),
        )

    def sq_start(d, carry):
        sq_copy(d).start()
        return carry

    lax.fori_loop(1, owners, sq_start, 0)

    launch(0)

    def sq_wait(d, tot):
        sq_copy(d).wait_recv()
        return tot + sq[d]

    total = lax.fori_loop(1, owners, sq_wait, sq[0])
    total = jnp.broadcast_to(jnp.sum(total, axis=(0, 1), keepdims=True), (TILE, ch))
    sq_out[core] = total

    norm = 1.0 / jnp.sqrt(total[0:1] / param_count + 1e-06)
    g_hat = both * norm
    mom = 0.9 * mw[0] + 0.1 * g_hat
    scaled = mw[1]

    def unit(h, carry):
        r0, r1 = carry
        v = w_in[h, 0] * g_hat + w_in[h, 1] * mom
        v = v + w_in[h, 2] * scaled + b_in[h]
        u = v * (1.0 / (1.0 + jnp.exp(-v)))
        return r0 + w_out[0, h] * u, r1 + w_out[1, h] * u

    zero = jnp.zeros((count, ch), F32)
    r0, r1 = lax.fori_loop(0, b_in.shape[0], unit, (zero, zero), unroll=4)
    update = (r0 + b_out[0]) * jnp.exp(jnp.tanh(r1 + b_out[1]))
    for part in parts:
        upd_out[core, own[part]] = update[part * chunk : (part + 1) * chunk]
    launch(1)

    sq_final = remote(
        sq_out.at[core], sq_out.at[core], sq_send.at[0], sq_recv.at[0], (other, col)
    )
    sq_final.start()
    sent.append(sq_final)

    for step in reversed(range(steps)):
        for k in range(2):
            for part in parts:
                collect(k, part)
                if step > 0:
                    spread(k, part, step - 1)
    for k, flat in enumerate((grads_flat, upd_flat)):
        for c in landing[k]:
            c.wait_recv()
        for layer in range(2):
            for part in parts:
                flat[pl.ds(2 * part * true + layer, true, stride=2), :] = outs[k][
                    layer, pl.ds(base[part], true)
                ]
    sq_final.wait_recv()
    for c in sent:
        c.wait_send()

    def sq_done(d, carry):
        sq_copy(d).wait_send()
        return carry

    lax.fori_loop(1, owners, sq_done, 0)


def on_device(
    rows_axis, cols_axis,
    features, cotangent, kernels, momentum, mlp_in_weight, mlp_in_bias, mlp_out_weight, mlp_out_bias,
):
    tile_rows, tile_cols, ch = features.shape
    param_count = 9 * ch * ch
    gain = math.sqrt(9.0 * ch)
    true, padded, orders, chunk = plan(rows_axis, cols_axis, ch)
    row, col = lax.axis_index("row"), lax.axis_index("col")
    steps = len(orders[0])
    owners = (rows_axis // 2) * cols_axis
    length = 3 * padded

    def shard(values, unit):
        pieces = []
        for part in range(3):
            at = place(row, col, cols_axis, orders[part], padded)
            if padded > true:
                cut = values[:, part * true * unit : (part + 1) * true * unit]
                pads = ((0, 0), (0, (padded - true) * unit)) + ((0, 0),) * (values.ndim - 2)
                cut = jnp.pad(cut, pads)
            else:
                cut, at = values, at + part * true
            start = (row % 2, at * unit) + (0,) * (values.ndim - 2)
            piece = lax.dynamic_slice(cut, start, (1, chunk * unit) + values.shape[2:])
            pieces.append(piece.reshape(chunk, ch).astype(F32))
        return jnp.concatenate(pieces, axis=0)

    mw = jnp.stack([shard(momentum, ch), shard(kernels.reshape(2, 9 * ch, ch), 1) * gain])
    cfg = (rows_axis, cols_axis, float(param_count), true, padded, orders, chunk)
    vmem = pl.BlockSpec(memory_space=pltpu.VMEM)
    smem = pl.BlockSpec(memory_space=pltpu.SMEM)
    dma = pltpu.SemaphoreType.DMA
    full = (length, ch)
    grads, update, squares = pl.pallas_call(
        functools.partial(step_kernel, cfg),
        out_shape=(
            jax.ShapeDtypeStruct((18 * ch, ch), F32),
            jax.ShapeDtypeStruct((18 * ch, ch), F32),
            jax.ShapeDtypeStruct((2, TILE, ch), F32),
        ),
        in_specs=[vmem] * 4 + [smem] * 4,
        out_specs=(vmem,) * 3,
        scratch_shapes=[
            pltpu.VMEM((2, 2, tile_rows, ch), BF16),
            pltpu.VMEM((2, 2, tile_cols, ch), BF16),
            pltpu.VMEM((2, 2, tile_rows, ch), BF16),
            pltpu.VMEM((2, 4, 16, ch), BF16),
            pltpu.VMEM(((tile_rows + 2) * tile_cols, 3 * ch), BF16),
            pltpu.VMEM(((tile_rows + 2) * tile_cols, 3 * ch), BF16),
            pltpu.VMEM((tile_rows * tile_cols, ch), BF16),
            pltpu.VMEM((tile_rows * tile_cols, ch), BF16),
            pltpu.VMEM((2,) + full, F32),
            pltpu.VMEM(full, F32),
            pltpu.VMEM(full, F32),
            pltpu.VMEM(full, F32),
            pltpu.VMEM((owners, TILE, ch), F32),
            pltpu.VMEM((2,) + full, F32),
            pltpu.VMEM((2,) + full, F32),
            dma((2, 8)), dma((2, 8)),
            dma((3,)), dma((3,)),
            dma((3, steps, cols_axis)), dma((3, steps, cols_axis)),
            dma((owners,)), dma((owners,)),
            dma((2, 3, steps, cols_axis)), dma((2, 3, steps, cols_axis)),
            dma((2, 3, steps + 1, cols_axis)), dma((2, 3, steps + 1, cols_axis)),
        ],
        compiler_params=pltpu.CompilerParams(
            collective_id=0, has_side_effects=True, vmem_limit_bytes=48 * 2**20
        ),
    )(
        features, cotangent, kernels.reshape(2, 9 * ch, ch), mw,
        mlp_in_weight, mlp_in_bias, mlp_out_weight, mlp_out_bias,
    )

    def flat(values):
        return values.reshape(9 * ch, 2, ch).transpose(1, 0, 2).reshape(2, param_count)

    norm = 1.0 / jnp.sqrt(squares[:, 0, :1] / float(param_count) + 1e-06)
    momentum_out = 0.9 * momentum + 0.1 * (flat(grads) * norm)
    return flat(update), momentum_out


def solution(mesh):
    placed = (P("row", "col", None), P("row", "col", None), P(), P(), P(), P(), P(), P())
    return jax.shard_map(
        functools.partial(on_device, mesh.shape["row"], mesh.shape["col"]),
        mesh=mesh, in_specs=placed, out_specs=(P(), P()), check_vma=False,
    )
```

```python
import functools
import math

import jax
import jax.numpy as jnp
from jax import lax
from jax.experimental import pallas as pl
from jax.experimental.pallas import tpu as pltpu
from jax.sharding import PartitionSpec as P

MESH = pl.DeviceIdType.MESH
TILE = 8
F32 = jnp.float32
BF16 = jnp.bfloat16


def plan(rows_axis, cols_axis, channels):
    bits = rows_axis.bit_length() - 1
    owners = (rows_axis // 2) * cols_axis
    true = 3 * channels
    padded = -(-true // (owners * TILE)) * owners * TILE
    stages = list(range(1, bits)) + [None]
    orders = tuple(tuple(stages[p:] + stages[:p]) for p in (0, 1, len(stages) - 1))
    return true, padded, orders, padded // owners


def place(row, col, cols_axis, order, total):
    off = 0
    for bit in order:
        if bit is None:
            total //= cols_axis
            off = off + col * total
        else:
            total //= 2
            off = off + ((row // 2**bit) % 2) * total
    return off


def step_kernel(
    cfg,
    feat_hbm, cot_hbm, ker_hbm, mom_hbm, w_in_hbm, b_in_hbm, w_out_hbm, b_out_hbm,
    grads_flat, upd_flat, sq_out,
    feat, cot, ker, mom_in, ker_in, w_in, b_in, w_out, b_out, load_sem,
    edge, ns, we, cr, x3, y3, hid, pg, g, rc, s, rb, sq, grads_out, upd_out,
    halo_send, halo_recv, core_send, core_recv, rs_send, rs_recv, sq_send, sq_recv,
    ag_send, ag_recv, fw_send, fw_recv,
):
    rows_axis, cols_axis, param_count, true, padded, orders, chunk = cfg
    tile_rows, tile_cols, ch = feat.shape
    cells = tile_rows * tile_cols
    row, col = lax.axis_index("row"), lax.axis_index("col")
    core = row % 2
    other = row + 1 - 2 * core
    devices = rows_axis * cols_axis
    base = (0, padded, 2 * padded)
    parts = range(3)

    def remote(src, dst, send, recv, to):
        return pltpu.make_async_remote_copy(
            src_ref=src, dst_ref=dst, send_sem=send, recv_sem=recv,
            device_id=to, device_id_type=MESH,
        )

    loads = [
        pltpu.make_async_copy(src, dst, load_sem.at[i])
        for i, (src, dst) in enumerate((
            (feat_hbm, feat), (cot_hbm, cot), (ker_hbm, ker), (w_in_hbm, w_in),
            (b_in_hbm, b_in), (w_out_hbm, w_out), (b_out_hbm, b_out),
        ))
    ]
    for part in parts:
        at = place(row, col, cols_axis, orders[part], padded)
        if padded > true:
            at = at % true
        at = pl.multiple_of(part * true + at, TILE)
        twice = pl.multiple_of(2 * at, 2 * TILE)
        loads.append(pltpu.make_async_copy(
            mom_hbm.at[pl.ds(twice, 2 * chunk)], mom_in.at[part], load_sem.at[7 + part]
        ))
        loads.append(pltpu.make_async_copy(
            ker_hbm.at[core, pl.ds(at, chunk)], ker_in.at[part], load_sem.at[10 + part]
        ))
    for copy in loads:
        copy.start()
    for copy in loads[:2]:
        copy.wait()
    for i, ref in enumerate((feat, cot)):
        edge[i, 0] = ref[:, 0:16, :].astype(F32)[:, 0, :].astype(BF16)
        edge[i, 1] = ref[:, tile_cols - 16 :, :].astype(F32)[:, 15, :].astype(BF16)

    barrier = pltpu.get_barrier_semaphore()
    here = row * cols_axis + col

    def greet(d, carry):
        t = (here + d) % devices
        pl.semaphore_signal(
            barrier, inc=1, device_id=(t // cols_axis, t % cols_axis), device_id_type=MESH
        )
        return carry

    lax.fori_loop(1, devices, greet, 0)
    pl.semaphore_wait(barrier, devices - 1)

    up, down = (row + rows_axis - 1) % rows_axis, (row + 1) % rows_axis
    west, east = (col + cols_axis - 1) % cols_axis, (col + 1) % cols_axis
    last = tile_rows - 1
    halos = []
    for i, ref in enumerate((feat, cot)):
        lo, hi = pl.ds(0, 16), pl.ds(tile_cols - 16, 16)
        moves = (
            (ref.at[last], ns.at[i, 0], (down, col)),
            (ref.at[0], ns.at[i, 1], (up, col)),
            (edge.at[i, 1], we.at[i, 0], (row, east)),
            (edge.at[i, 0], we.at[i, 1], (row, west)),
            (ref.at[last, hi], cr.at[i, 0], (down, east)),
            (ref.at[last, lo], cr.at[i, 1], (down, west)),
            (ref.at[0, hi], cr.at[i, 2], (up, east)),
            (ref.at[0, lo], cr.at[i, 3], (up, west)),
        )
        mine = [
            remote(src, dst, halo_send.at[i, k], halo_recv.at[i, k], to)
            for k, (src, dst, to) in enumerate(moves)
        ]
        for copy in mine:
            copy.start()
        halos.append(mine)

    def put(dst, first, v, w, e):
        n = v.shape[0]
        at = lax.broadcasted_iota(jnp.int32, v.shape, 1)
        left = jnp.where(at == 0, w[:, None, :], pltpu.roll(v, 1, 1))
        right = jnp.where(at == tile_cols - 1, e[:, None, :], pltpu.roll(v, tile_cols - 1, 1))
        span = pl.ds(first * tile_cols, n * tile_cols)
        for b, part in enumerate((left, v, right)):
            dst[span, b * ch : (b + 1) * ch] = part.reshape(n * tile_cols, ch).astype(BF16)

    def build(i, ref, dst):
        for copy in halos[i]:
            copy.wait_recv()
        put(dst, 0, ns[i, 0].astype(F32)[None], cr[i, 0].astype(F32)[15:16], cr[i, 1].astype(F32)[0:1])
        for r in range(0, tile_rows, 16):
            span = pl.ds(r, 16)
            put(dst, r + 1, ref[span].astype(F32), we[i, 0, span].astype(F32), we[i, 1, span].astype(F32))
        put(
            dst, tile_rows + 1,
            ns[i, 1].astype(F32)[None], cr[i, 2].astype(F32)[15:16], cr[i, 3].astype(F32)[0:1],
        )

    build(0, feat, x3)
    build(1, cot, y3)

    loads[2].wait()
    flip = [
        jnp.concatenate([ker[1, (3 * a + b) * ch : (3 * a + b + 1) * ch] for b in (2, 1, 0)], axis=1)
        for a in range(3)
    ]
    block = min(cells, 512)
    for m in range(0, cells, block):
        pre = jnp.zeros((block, ch), F32)
        back = jnp.zeros((block, ch), F32)
        for a in range(3):
            pre += jnp.dot(
                x3[pl.ds(m + a * tile_cols, block)],
                ker[0, 3 * a * ch : 3 * (a + 1) * ch],
                preferred_element_type=F32,
            )
            back += lax.dot_general(
                y3[pl.ds(m + (2 - a) * tile_cols, block)], flip[a],
                (((1,), (1,)), ((), ())), preferred_element_type=F32,
            )
        sig = 1.0 / (1.0 + jnp.exp(-pre))
        hid[pl.ds(m, block)] = (pre * sig).astype(BF16)
        pg[pl.ds(m, block)] = (back * sig * (1.0 + pre * (1.0 - sig))).astype(BF16)

    def tap_rows(t):
        return pl.ds(base[t // 3] + (t % 3) * ch, ch)

    if padded > true:
        for part in parts:
            for layer in range(2):
                g[layer, pl.ds(base[part] + true, padded - true)] = jnp.zeros((padded - true, ch), F32)

    sent = [copy for mine in halos for copy in mine]
    swaps = []
    hid_t, pg_t = hid[...].T, pg[...].T
    for a in parts:
        two = jnp.dot(hid_t, y3[pl.ds((2 - a) * tile_cols, cells)], preferred_element_type=F32)
        one = jnp.dot(pg_t, x3[pl.ds(a * tile_cols, cells)], preferred_element_type=F32)
        for b in range(3):
            g[1, tap_rows(3 * a + 2 - b)] = two[:, b * ch : (b + 1) * ch]
            g[0, tap_rows(3 * a + b)] = one[:, b * ch : (b + 1) * ch].T
        span = pl.ds(base[a], padded)
        copy = remote(
            g.at[1 - core, span], rc.at[span], core_send.at[a], core_recv.at[a], (other, col)
        )
        copy.start()
        swaps.append(copy)
    sent += swaps

    off, size, slot = list(base), [padded] * 3, list(base)
    steps = len(orders[0])
    pending = [None] * 3

    def rows_at(start, n):
        return pl.ds(pl.multiple_of(start, TILE), n)

    def begin(part, step):
        bit = orders[part][step]
        if bit is None:
            n = size[part] // cols_axis
            peers = [
                (d, off[part] + ((col + d) % cols_axis) * n, (row, (col + d) % cols_axis))
                for d in range(1, cols_axis)
            ]
            off[part] = off[part] + col * n
        else:
            n = size[part] // 2
            side = (row // 2**bit) % 2
            peers = [(0, off[part] + (1 - side) * n, (row + (1 - 2 * side) * 2**bit, col))]
            off[part] = off[part] + side * n
        size[part] = n
        pending[part] = []
        for d, start, to in peers:
            into = pl.ds(slot[part], n)
            slot[part] += n
            copy = remote(
                s.at[rows_at(start, n)], rb.at[into],
                rs_send.at[part, step, d], rs_recv.at[part, step, d], to,
            )
            copy.start()
            sent.append(copy)
            pending[part].append((copy, into))

    for part in parts:
        swaps[part].wait_recv()
        span = pl.ds(base[part], padded)
        s[span] = g[core, span] + rc[span]
        begin(part, 0)
    own, mine = [], []
    for step in range(steps):
        for part in parts:
            at = rows_at(off[part], size[part])
            total = s[at]
            for copy, into in pending[part]:
                copy.wait_recv()
                total += rb[into]
            if step + 1 < steps:
                s[at] = total
                begin(part, step + 1)
            else:
                grads_out[core, at] = total
                own.append(at)
                mine.append(total)

    outs = (grads_out, upd_out)
    offs, sizes = [list(off), list(off)], [list(size), list(size)]
    flight = [[None] * 3, [None] * 3]
    landing = [[], []]

    def forward(k, part, step, d, at):
        c = remote(
            outs[k].at[core, at], outs[k].at[core, at],
            fw_send.at[k, part, step, d], fw_recv.at[k, part, step, d], (other, col),
        )
        c.start()
        sent.append(c)
        landing[k].append(c)

    def spread(k, part, step):
        bit = orders[part][step]
        n, first = sizes[k][part], offs[k][part]
        here_at = rows_at(first, n)
        if bit is None:
            whole = first - col * n
            peers = [
                (d, (row, (col + d) % cols_axis), whole + ((col + cols_axis - d) % cols_axis) * n)
                for d in range(1, cols_axis)
            ]
            offs[k][part], sizes[k][part] = whole, n * cols_axis
        else:
            side = (row // 2**bit) % 2
            whole = first - side * n
            peers = [(0, (row + (1 - 2 * side) * 2**bit, col), whole + (1 - side) * n)]
            offs[k][part], sizes[k][part] = whole, 2 * n
        flight[k][part] = []
        for d, to, arrives in peers:
            c = remote(
                outs[k].at[core, here_at], outs[k].at[core, here_at],
                ag_send.at[k, part, step, d], ag_recv.at[k, part, step, d], to,
            )
            c.start()
            sent.append(c)
            flight[k][part].append((c, step, d, rows_at(arrives, n)))

    def collect(k, part):
        for c, step, d, at in flight[k][part]:
            c.wait_recv()
            forward(k, part, step, d, at)

    def launch(k):
        for part in parts:
            spread(k, part, steps - 1)
        for part in parts:
            forward(k, part, steps, 0, own[part])

    both = jnp.concatenate(mine, axis=0)
    count = 3 * chunk
    sq[0] = jnp.sum((both * both).reshape(count // TILE, TILE, ch), axis=0)
    owners = (rows_axis // 2) * cols_axis
    me = (row // 2) * cols_axis + col

    def sq_copy(d):
        t = (me + d) % owners
        return remote(
            sq.at[0], sq.at[d], sq_send.at[d], sq_recv.at[d],
            (2 * (t // cols_axis) + core, t % cols_axis),
        )

    def sq_start(d, carry):
        sq_copy(d).start()
        return carry

    lax.fori_loop(1, owners, sq_start, 0)

    launch(0)

    def sq_wait(d, tot):
        sq_copy(d).wait_recv()
        return tot + sq[d]

    total = lax.fori_loop(1, owners, sq_wait, sq[0])
    total = jnp.broadcast_to(jnp.sum(total, axis=(0, 1), keepdims=True), (TILE, ch))
    sq_out[core] = total

    for copy in loads[3:]:
        copy.wait()
    momentum = jnp.concatenate(
        [mom_in[part, pl.ds(core, chunk, stride=2), :] for part in parts], axis=0
    )
    scaled = jnp.concatenate([ker_in[part].astype(F32) for part in parts], axis=0)
    scaled = scaled * math.sqrt(9.0 * ch)
    norm = 1.0 / jnp.sqrt(total[0:1] / param_count + 1e-06)
    g_hat = both * norm
    mom = 0.9 * momentum + 0.1 * g_hat

    def unit(h, carry):
        r0, r1 = carry
        v = w_in[0, h] * g_hat + w_in[1, h] * mom
        v = v + w_in[2, h] * scaled + b_in[h]
        u = v * (1.0 / (1.0 + jnp.exp(-v)))
        return r0 + w_out[0, h] * u, r1 + w_out[1, h] * u

    zero = jnp.zeros((count, ch), F32)
    r0, r1 = lax.fori_loop(0, b_in.shape[0], unit, (zero, zero), unroll=4)
    update = (r0 + b_out[0]) * jnp.exp(jnp.tanh(r1 + b_out[1]))
    for part in parts:
        upd_out[core, own[part]] = update[part * chunk : (part + 1) * chunk]
    launch(1)

    sq_final = remote(
        sq_out.at[core], sq_out.at[core], sq_send.at[0], sq_recv.at[0], (other, col)
    )
    sq_final.start()
    sent.append(sq_final)

    for step in reversed(range(steps)):
        for k in range(2):
            for part in parts:
                collect(k, part)
                if step > 0:
                    spread(k, part, step - 1)
    for k, flat in enumerate((grads_flat, upd_flat)):
        for c in landing[k]:
            c.wait_recv()
        for layer in range(2):
            for part in parts:
                flat[pl.ds(2 * part * true + layer, true, stride=2), :] = outs[k][
                    layer, pl.ds(base[part], true)
                ]
    sq_final.wait_recv()
    for c in sent:
        c.wait_send()

    def sq_done(d, carry):
        sq_copy(d).wait_send()
        return carry

    lax.fori_loop(1, owners, sq_done, 0)


def on_device(
    rows_axis, cols_axis,
    features, cotangent, kernels, momentum, mlp_in_weight, mlp_in_bias, mlp_out_weight, mlp_out_bias,
):
    tile_rows, tile_cols, ch = features.shape
    param_count = 9 * ch * ch
    true, padded, orders, chunk = plan(rows_axis, cols_axis, ch)
    steps = len(orders[0])
    owners = (rows_axis // 2) * cols_axis
    length = 3 * padded

    cfg = (rows_axis, cols_axis, float(param_count), true, padded, orders, chunk)
    vmem = pl.BlockSpec(memory_space=pltpu.VMEM)
    hbm = pl.BlockSpec(memory_space=pltpu.HBM)
    hidden_units = mlp_in_bias.shape[0]
    dma = pltpu.SemaphoreType.DMA
    full = (length, ch)
    grads, update, squares = pl.pallas_call(
        functools.partial(step_kernel, cfg),
        out_shape=(
            jax.ShapeDtypeStruct((18 * ch, ch), F32),
            jax.ShapeDtypeStruct((18 * ch, ch), F32),
            jax.ShapeDtypeStruct((2, TILE, ch), F32),
        ),
        in_specs=[hbm] * 8,
        out_specs=(vmem,) * 3,
        scratch_shapes=[
            pltpu.VMEM(features.shape, BF16),
            pltpu.VMEM(cotangent.shape, BF16),
            pltpu.VMEM((2, 9 * ch, ch), BF16),
            pltpu.VMEM((3, 2 * chunk, ch), F32),
            pltpu.VMEM((3, chunk, ch), BF16),
            pltpu.SMEM((3, hidden_units), F32),
            pltpu.SMEM((hidden_units,), F32),
            pltpu.SMEM((2, hidden_units), F32),
            pltpu.SMEM((2,), F32),
            dma((13,)),
            pltpu.VMEM((2, 2, tile_rows, ch), BF16),
            pltpu.VMEM((2, 2, tile_cols, ch), BF16),
            pltpu.VMEM((2, 2, tile_rows, ch), BF16),
            pltpu.VMEM((2, 4, 16, ch), BF16),
            pltpu.VMEM(((tile_rows + 2) * tile_cols, 3 * ch), BF16),
            pltpu.VMEM(((tile_rows + 2) * tile_cols, 3 * ch), BF16),
            pltpu.VMEM((tile_rows * tile_cols, ch), BF16),
            pltpu.VMEM((tile_rows * tile_cols, ch), BF16),
            pltpu.VMEM((2,) + full, F32),
            pltpu.VMEM(full, F32),
            pltpu.VMEM(full, F32),
            pltpu.VMEM(full, F32),
            pltpu.VMEM((owners, TILE, ch), F32),
            pltpu.VMEM((2,) + full, F32),
            pltpu.VMEM((2,) + full, F32),
            dma((2, 8)), dma((2, 8)),
            dma((3,)), dma((3,)),
            dma((3, steps, cols_axis)), dma((3, steps, cols_axis)),
            dma((owners,)), dma((owners,)),
            dma((2, 3, steps, cols_axis)), dma((2, 3, steps, cols_axis)),
            dma((2, 3, steps + 1, cols_axis)), dma((2, 3, steps + 1, cols_axis)),
        ],
        compiler_params=pltpu.CompilerParams(
            collective_id=0, has_side_effects=True, vmem_limit_bytes=64600000
        ),
    )(
        features, cotangent, kernels.reshape(2, 9 * ch, ch),
        momentum.reshape(2, 9 * ch, ch).transpose(1, 0, 2).reshape(18 * ch, ch),
        mlp_in_weight.T, mlp_in_bias, mlp_out_weight, mlp_out_bias,
    )

    def flat(values):
        return values.reshape(9 * ch, 2, ch).transpose(1, 0, 2).reshape(2, param_count)

    norm = 1.0 / jnp.sqrt(squares[:, 0, :1] / float(param_count) + 1e-06)
    momentum_out = 0.9 * momentum + 0.1 * (flat(grads) * norm)
    return flat(update), momentum_out


def solution(mesh):
    placed = (P("row", "col", None), P("row", "col", None), P(), P(), P(), P(), P(), P())
    return jax.shard_map(
        functools.partial(on_device, mesh.shape["row"], mesh.shape["col"]),
        mesh=mesh, in_specs=placed, out_specs=(P(), P()), check_vma=False,
    )
```

```python
import functools
import math

import jax
import jax.numpy as jnp
from jax import lax
from jax.experimental import pallas as pl
from jax.experimental.pallas import tpu as pltpu
from jax.sharding import PartitionSpec as P

MESH = pl.DeviceIdType.MESH
TILE = 8
F32 = jnp.float32
BF16 = jnp.bfloat16


def plan(rows_axis, cols_axis, channels):
    bits = rows_axis.bit_length() - 1
    owners = (rows_axis // 2) * cols_axis
    true = 3 * channels
    padded = -(-true // (owners * TILE)) * owners * TILE
    stages = list(range(1, bits)) + [None]
    orders = tuple(tuple(stages[p:] + stages[:p]) for p in (0, 1, len(stages) - 1))
    return true, padded, orders, padded // owners


def place(row, col, cols_axis, order, total):
    off = 0
    for bit in order:
        if bit is None:
            total //= cols_axis
            off = off + col * total
        else:
            total //= 2
            off = off + ((row // 2**bit) % 2) * total
    return off


def step_kernel(
    cfg,
    feat_hbm, cot_hbm, ker_hbm, mom_hbm, w_in_hbm, b_in_hbm, w_out_hbm, b_out_hbm,
    mom_flat, upd_flat,
    feat, cot, ker, mom_in, ker_in, w_in, b_in, w_out, b_out, load_sem,
    mom_all, sq_out, edge, ns, we, cr, x3, y3, hid, pg, g, rc, s, rb, sq, grads_out, upd_out,
    halo_send, halo_recv, core_send, core_recv, rs_send, rs_recv, sq_send, sq_recv,
    ag_send, ag_recv, fw_send, fw_recv,
):
    rows_axis, cols_axis, param_count, true, padded, orders, chunk = cfg
    tile_rows, tile_cols, ch = feat.shape
    cells = tile_rows * tile_cols
    row, col = lax.axis_index("row"), lax.axis_index("col")
    core = row % 2
    other = row + 1 - 2 * core
    devices = rows_axis * cols_axis
    base = (0, padded, 2 * padded)
    parts = range(3)

    def remote(src, dst, send, recv, to):
        return pltpu.make_async_remote_copy(
            src_ref=src, dst_ref=dst, send_sem=send, recv_sem=recv,
            device_id=to, device_id_type=MESH,
        )

    loads = [
        pltpu.make_async_copy(src, dst, load_sem.at[i])
        for i, (src, dst) in enumerate((
            (feat_hbm, feat), (cot_hbm, cot), (ker_hbm, ker), (w_in_hbm, w_in),
            (b_in_hbm, b_in), (w_out_hbm, w_out), (b_out_hbm, b_out), (mom_hbm, mom_all),
        ))
    ]
    for part in parts:
        at = place(row, col, cols_axis, orders[part], padded)
        if padded > true:
            at = at % true
        at = pl.multiple_of(part * true + at, TILE)
        twice = pl.multiple_of(2 * at, 2 * TILE)
        loads.append(pltpu.make_async_copy(
            mom_hbm.at[pl.ds(twice, 2 * chunk)], mom_in.at[part], load_sem.at[8 + part]
        ))
        loads.append(pltpu.make_async_copy(
            ker_hbm.at[core, pl.ds(at, chunk)], ker_in.at[part], load_sem.at[11 + part]
        ))
    for copy in loads:
        copy.start()
    for copy in loads[:2]:
        copy.wait()
    for i, ref in enumerate((feat, cot)):
        edge[i, 0] = ref[:, 0:16, :].astype(F32)[:, 0, :].astype(BF16)
        edge[i, 1] = ref[:, tile_cols - 16 :, :].astype(F32)[:, 15, :].astype(BF16)

    barrier = pltpu.get_barrier_semaphore()
    here = row * cols_axis + col

    def greet(d, carry):
        t = (here + d) % devices
        pl.semaphore_signal(
            barrier, inc=1, device_id=(t // cols_axis, t % cols_axis), device_id_type=MESH
        )
        return carry

    lax.fori_loop(1, devices, greet, 0)
    pl.semaphore_wait(barrier, devices - 1)

    up, down = (row + rows_axis - 1) % rows_axis, (row + 1) % rows_axis
    west, east = (col + cols_axis - 1) % cols_axis, (col + 1) % cols_axis
    last = tile_rows - 1
    halos = []
    for i, ref in enumerate((feat, cot)):
        lo, hi = pl.ds(0, 16), pl.ds(tile_cols - 16, 16)
        moves = (
            (ref.at[last], ns.at[i, 0], (down, col)),
            (ref.at[0], ns.at[i, 1], (up, col)),
            (edge.at[i, 1], we.at[i, 0], (row, east)),
            (edge.at[i, 0], we.at[i, 1], (row, west)),
            (ref.at[last, hi], cr.at[i, 0], (down, east)),
            (ref.at[last, lo], cr.at[i, 1], (down, west)),
            (ref.at[0, hi], cr.at[i, 2], (up, east)),
            (ref.at[0, lo], cr.at[i, 3], (up, west)),
        )
        mine = [
            remote(src, dst, halo_send.at[i, k], halo_recv.at[i, k], to)
            for k, (src, dst, to) in enumerate(moves)
        ]
        for copy in mine:
            copy.start()
        halos.append(mine)

    def put(dst, first, v, w, e):
        n = v.shape[0]
        at = lax.broadcasted_iota(jnp.int32, v.shape, 1)
        left = jnp.where(at == 0, w[:, None, :], pltpu.roll(v, 1, 1))
        right = jnp.where(at == tile_cols - 1, e[:, None, :], pltpu.roll(v, tile_cols - 1, 1))
        span = pl.ds(first * tile_cols, n * tile_cols)
        for b, part in enumerate((left, v, right)):
            dst[span, b * ch : (b + 1) * ch] = part.reshape(n * tile_cols, ch).astype(BF16)

    def build(i, ref, dst):
        for copy in halos[i]:
            copy.wait_recv()
        put(dst, 0, ns[i, 0].astype(F32)[None], cr[i, 0].astype(F32)[15:16], cr[i, 1].astype(F32)[0:1])
        for r in range(0, tile_rows, 16):
            span = pl.ds(r, 16)
            put(dst, r + 1, ref[span].astype(F32), we[i, 0, span].astype(F32), we[i, 1, span].astype(F32))
        put(
            dst, tile_rows + 1,
            ns[i, 1].astype(F32)[None], cr[i, 2].astype(F32)[15:16], cr[i, 3].astype(F32)[0:1],
        )

    build(0, feat, x3)
    build(1, cot, y3)

    loads[2].wait()
    flip = [
        jnp.concatenate([ker[1, (3 * a + b) * ch : (3 * a + b + 1) * ch] for b in (2, 1, 0)], axis=1)
        for a in range(3)
    ]
    block = min(cells, 512)
    for m in range(0, cells, block):
        pre = jnp.zeros((block, ch), F32)
        back = jnp.zeros((block, ch), F32)
        for a in range(3):
            pre += jnp.dot(
                x3[pl.ds(m + a * tile_cols, block)],
                ker[0, 3 * a * ch : 3 * (a + 1) * ch],
                preferred_element_type=F32,
            )
            back += lax.dot_general(
                y3[pl.ds(m + (2 - a) * tile_cols, block)], flip[a],
                (((1,), (1,)), ((), ())), preferred_element_type=F32,
            )
        sig = 1.0 / (1.0 + jnp.exp(-pre))
        hid[pl.ds(m, block)] = (pre * sig).astype(BF16)
        pg[pl.ds(m, block)] = (back * sig * (1.0 + pre * (1.0 - sig))).astype(BF16)

    def tap_rows(t):
        return pl.ds(base[t // 3] + (t % 3) * ch, ch)

    if padded > true:
        for part in parts:
            for layer in range(2):
                g[layer, pl.ds(base[part] + true, padded - true)] = jnp.zeros((padded - true, ch), F32)

    sent = [copy for mine in halos for copy in mine]
    swaps = []
    hid_t, pg_t = hid[...].T, pg[...].T
    for a in parts:
        two = jnp.dot(hid_t, y3[pl.ds((2 - a) * tile_cols, cells)], preferred_element_type=F32)
        one = jnp.dot(pg_t, x3[pl.ds(a * tile_cols, cells)], preferred_element_type=F32)
        for b in range(3):
            g[1, tap_rows(3 * a + 2 - b)] = two[:, b * ch : (b + 1) * ch]
            g[0, tap_rows(3 * a + b)] = one[:, b * ch : (b + 1) * ch].T
        span = pl.ds(base[a], padded)
        copy = remote(
            g.at[1 - core, span], rc.at[span], core_send.at[a], core_recv.at[a], (other, col)
        )
        copy.start()
        swaps.append(copy)
    sent += swaps

    off, size, slot = list(base), [padded] * 3, list(base)
    steps = len(orders[0])
    pending = [None] * 3

    def rows_at(start, n):
        return pl.ds(pl.multiple_of(start, TILE), n)

    def begin(part, step):
        bit = orders[part][step]
        if bit is None:
            n = size[part] // cols_axis
            peers = [
                (d, off[part] + ((col + d) % cols_axis) * n, (row, (col + d) % cols_axis))
                for d in range(1, cols_axis)
            ]
            off[part] = off[part] + col * n
        else:
            n = size[part] // 2
            side = (row // 2**bit) % 2
            peers = [(0, off[part] + (1 - side) * n, (row + (1 - 2 * side) * 2**bit, col))]
            off[part] = off[part] + side * n
        size[part] = n
        pending[part] = []
        for d, start, to in peers:
            into = pl.ds(slot[part], n)
            slot[part] += n
            copy = remote(
                s.at[rows_at(start, n)], rb.at[into],
                rs_send.at[part, step, d], rs_recv.at[part, step, d], to,
            )
            copy.start()
            sent.append(copy)
            pending[part].append((copy, into))

    for part in parts:
        swaps[part].wait_recv()
        span = pl.ds(base[part], padded)
        s[span] = g[core, span] + rc[span]
        begin(part, 0)
    own, mine = [], []
    for step in range(steps):
        for part in parts:
            at = rows_at(off[part], size[part])
            total = s[at]
            for copy, into in pending[part]:
                copy.wait_recv()
                total += rb[into]
            if step + 1 < steps:
                s[at] = total
                begin(part, step + 1)
            else:
                grads_out[core, at] = total
                own.append(at)
                mine.append(total)

    outs = (grads_out, upd_out)
    offs, sizes = [list(off), list(off)], [list(size), list(size)]
    flight = [[None] * 3, [None] * 3]
    landing = [[], []]

    def forward(k, part, step, d, at):
        c = remote(
            outs[k].at[core, at], outs[k].at[core, at],
            fw_send.at[k, part, step, d], fw_recv.at[k, part, step, d], (other, col),
        )
        c.start()
        sent.append(c)
        landing[k].append(c)

    def spread(k, part, step):
        bit = orders[part][step]
        n, first = sizes[k][part], offs[k][part]
        here_at = rows_at(first, n)
        if bit is None:
            whole = first - col * n
            peers = [
                (d, (row, (col + d) % cols_axis), whole + ((col + cols_axis - d) % cols_axis) * n)
                for d in range(1, cols_axis)
            ]
            offs[k][part], sizes[k][part] = whole, n * cols_axis
        else:
            side = (row // 2**bit) % 2
            whole = first - side * n
            peers = [(0, (row + (1 - 2 * side) * 2**bit, col), whole + (1 - side) * n)]
            offs[k][part], sizes[k][part] = whole, 2 * n
        flight[k][part] = []
        for d, to, arrives in peers:
            c = remote(
                outs[k].at[core, here_at], outs[k].at[core, here_at],
                ag_send.at[k, part, step, d], ag_recv.at[k, part, step, d], to,
            )
            c.start()
            sent.append(c)
            flight[k][part].append((c, step, d, rows_at(arrives, n)))

    def collect(k, part):
        for c, step, d, at in flight[k][part]:
            c.wait_recv()
            forward(k, part, step, d, at)

    def launch(k):
        for part in parts:
            spread(k, part, steps - 1)
        for part in parts:
            forward(k, part, steps, 0, own[part])

    both = jnp.concatenate(mine, axis=0)
    count = 3 * chunk
    sq[0] = jnp.sum((both * both).reshape(count // TILE, TILE, ch), axis=0)
    owners = (rows_axis // 2) * cols_axis
    me = (row // 2) * cols_axis + col

    def sq_copy(d):
        t = (me + d) % owners
        return remote(
            sq.at[0], sq.at[d], sq_send.at[d], sq_recv.at[d],
            (2 * (t // cols_axis) + core, t % cols_axis),
        )

    def sq_start(d, carry):
        sq_copy(d).start()
        return carry

    lax.fori_loop(1, owners, sq_start, 0)

    launch(0)
    for part in parts:
        collect(0, part)
        if steps > 1:
            spread(0, part, steps - 2)

    def sq_wait(d, tot):
        sq_copy(d).wait_recv()
        return tot + sq[d]

    total = lax.fori_loop(1, owners, sq_wait, sq[0])
    total = jnp.broadcast_to(jnp.sum(total, axis=(0, 1), keepdims=True), (TILE, ch))
    sq_out[core] = total

    for copy in loads[3:]:
        copy.wait()
    momentum = jnp.concatenate(
        [mom_in[part, pl.ds(core, chunk, stride=2), :] for part in parts], axis=0
    )
    scaled = jnp.concatenate([ker_in[part].astype(F32) for part in parts], axis=0)
    scaled = scaled * math.sqrt(9.0 * ch)
    norm = 1.0 / jnp.sqrt(total[0:1] / param_count + 1e-06)
    g_hat = both * norm
    mom = 0.9 * momentum + 0.1 * g_hat

    def unit(h, carry):
        r0, r1 = carry
        v = w_in[0, h] * g_hat + w_in[1, h] * mom
        v = v + w_in[2, h] * scaled + b_in[h]
        u = v * (1.0 / (1.0 + jnp.exp(-v)))
        return r0 + w_out[0, h] * u, r1 + w_out[1, h] * u

    zero = jnp.zeros((count, ch), F32)
    r0, r1 = lax.fori_loop(0, b_in.shape[0], unit, (zero, zero), unroll=4)
    update = (r0 + b_out[0]) * jnp.exp(jnp.tanh(r1 + b_out[1]))
    for part in parts:
        upd_out[core, own[part]] = update[part * chunk : (part + 1) * chunk]
    launch(1)

    sq_final = remote(
        sq_out.at[core], sq_out.at[core], sq_send.at[0], sq_recv.at[0], (other, col)
    )
    sq_final.start()
    sent.append(sq_final)

    for step in reversed(range(steps)):
        for part in parts:
            if step >= 1:
                collect(0, part)
            if step >= 2:
                spread(0, part, step - 2)
        for part in parts:
            collect(1, part)
            if step >= 1:
                spread(1, part, step - 1)
    sq_final.wait_recv()
    for c in landing[0]:
        c.wait_recv()
    for layer in range(2):
        layer_norm = 1.0 / jnp.sqrt(sq_out[layer, 0:1] / param_count + 1e-06)
        for part in parts:
            at = pl.ds(2 * part * true + layer, true, stride=2)
            mom_flat[at, :] = 0.9 * mom_all[at, :] + 0.1 * (
                grads_out[layer, pl.ds(base[part], true)] * layer_norm
            )
    for c in landing[1]:
        c.wait_recv()
    for layer in range(2):
        for part in parts:
            at = pl.ds(2 * part * true + layer, true, stride=2)
            upd_flat[at, :] = upd_out[layer, pl.ds(base[part], true)]
    for c in sent:
        c.wait_send()

    def sq_done(d, carry):
        sq_copy(d).wait_send()
        return carry

    lax.fori_loop(1, owners, sq_done, 0)


def on_device(
    rows_axis, cols_axis,
    features, cotangent, kernels, momentum, mlp_in_weight, mlp_in_bias, mlp_out_weight, mlp_out_bias,
):
    tile_rows, tile_cols, ch = features.shape
    param_count = 9 * ch * ch
    true, padded, orders, chunk = plan(rows_axis, cols_axis, ch)
    steps = len(orders[0])
    owners = (rows_axis // 2) * cols_axis
    length = 3 * padded

    cfg = (rows_axis, cols_axis, float(param_count), true, padded, orders, chunk)
    vmem = pl.BlockSpec(memory_space=pltpu.VMEM)
    hbm = pl.BlockSpec(memory_space=pltpu.HBM)
    hidden_units = mlp_in_bias.shape[0]
    dma = pltpu.SemaphoreType.DMA
    full = (length, ch)
    moved, update = pl.pallas_call(
        functools.partial(step_kernel, cfg),
        out_shape=(
            jax.ShapeDtypeStruct((18 * ch, ch), F32),
            jax.ShapeDtypeStruct((18 * ch, ch), F32),
        ),
        in_specs=[hbm] * 8,
        out_specs=(vmem,) * 2,
        scratch_shapes=[
            pltpu.VMEM(features.shape, BF16),
            pltpu.VMEM(cotangent.shape, BF16),
            pltpu.VMEM((2, 9 * ch, ch), BF16),
            pltpu.VMEM((3, 2 * chunk, ch), F32),
            pltpu.VMEM((3, chunk, ch), BF16),
            pltpu.SMEM((3, hidden_units), F32),
            pltpu.SMEM((hidden_units,), F32),
            pltpu.SMEM((2, hidden_units), F32),
            pltpu.SMEM((2,), F32),
            dma((14,)),
            pltpu.VMEM((18 * ch, ch), F32),
            pltpu.VMEM((2, TILE, ch), F32),
            pltpu.VMEM((2, 2, tile_rows, ch), BF16),
            pltpu.VMEM((2, 2, tile_cols, ch), BF16),
            pltpu.VMEM((2, 2, tile_rows, ch), BF16),
            pltpu.VMEM((2, 4, 16, ch), BF16),
            pltpu.VMEM(((tile_rows + 2) * tile_cols, 3 * ch), BF16),
            pltpu.VMEM(((tile_rows + 2) * tile_cols, 3 * ch), BF16),
            pltpu.VMEM((tile_rows * tile_cols, ch), BF16),
            pltpu.VMEM((tile_rows * tile_cols, ch), BF16),
            pltpu.VMEM((2,) + full, F32),
            pltpu.VMEM(full, F32),
            pltpu.VMEM(full, F32),
            pltpu.VMEM(full, F32),
            pltpu.VMEM((owners, TILE, ch), F32),
            pltpu.VMEM((2,) + full, F32),
            pltpu.VMEM((2,) + full, F32),
            dma((2, 8)), dma((2, 8)),
            dma((3,)), dma((3,)),
            dma((3, steps, cols_axis)), dma((3, steps, cols_axis)),
            dma((owners,)), dma((owners,)),
            dma((2, 3, steps, cols_axis)), dma((2, 3, steps, cols_axis)),
            dma((2, 3, steps + 1, cols_axis)), dma((2, 3, steps + 1, cols_axis)),
        ],
        compiler_params=pltpu.CompilerParams(
            collective_id=0, has_side_effects=True, vmem_limit_bytes=64600000
        ),
    )(
        features, cotangent, kernels.reshape(2, 9 * ch, ch),
        momentum.reshape(2, 9 * ch, ch).transpose(1, 0, 2).reshape(18 * ch, ch),
        mlp_in_weight.T, mlp_in_bias, mlp_out_weight, mlp_out_bias,
    )

    def flat(values):
        return values.reshape(9 * ch, 2, ch).transpose(1, 0, 2).reshape(2, param_count)

    return flat(update), flat(moved)


def solution(mesh):
    placed = (P("row", "col", None), P("row", "col", None), P(), P(), P(), P(), P(), P())
    return jax.shard_map(
        functools.partial(on_device, mesh.shape["row"], mesh.shape["col"]),
        mesh=mesh, in_specs=placed, out_specs=(P(), P()), check_vma=False,
    )
```
